32 devices in a mesh: tm: 8 (over z, x), rows: 4 (over y, core).
Axes of the slice: x: 2, y: 2, z: 4, core: 2. Of those that a mesh axis runs over, the one named last changes fastest.
Arguments:
- latents: bfloat16 [32, 16, 32, 256], P('tm', 'rows'), may hold values from -6 to 6
- frame_gaps: float32 [32], P('tm'), may hold values from 0.5 to 250
- decay_rates: float32 [2, 256], replicated, may hold values from 0.0011 to 0.05
- input_kernel: bfloat16 [2, 3, 3, 256, 256], replicated, may hold values from -0.125 to 0.125
- output_kernel: bfloat16 [2, 3, 3, 256, 256], replicated, may hold values from -0.125 to 0.125
- feedthrough: float32 [2, 256], replicated, may hold values from -1 to 1
Outputs:
- encoded: bfloat16 [32, 16, 32, 256], P('tm', 'rows')
The draws below stay inside these ranges and needn't reach their ends.
All inputs are finite; a program needn't handle non-finite values.
Results may differ from the reference program's by a relative error of at most 0.012.
Values may be sent and summed in bfloat16 or wider, within the bound.
A program may use at most 64 MiB of HBM per device.

```python
import math
import jax
import jax.numpy as jnp
from jax import lax

C = 256
P_SIZE = 256
W = 32
STACK_COUNT = 2
FRAMES = 32
H = 16


def draw_frame_gaps(key, part):
    key_parent, seed_occurrences, key_positions = jax.random.split(jax.random.fold_in(key, 11), 3)
    snapshot_spacing = jnp.exp(jax.random.uniform(key_parent, (FRAMES,), jnp.float32, -0.69, 0.69))
    occurrence_locations = jax.random.permutation(key_positions, FRAMES)[:2]
    rapid_occurrences = jax.random.uniform(seed_occurrences, (2,), jnp.float32, 150.0, 250.0)
    return snapshot_spacing.at[occurrence_locations].set(rapid_occurrences)


def permute_channels(key_layer):
    return jax.random.permutation(key_layer, P_SIZE)


def draw_decay_rates(key, part):
    key_pick, key_fast, key_slow = jax.random.split(jax.random.fold_in(key, 23), 3)
    fast_rates = jax.random.uniform(key_fast, (STACK_COUNT, P_SIZE), jnp.float32, 0.03, 0.05)
    slow_rates = jnp.exp(jax.random.uniform(key_slow, (STACK_COUNT, P_SIZE), jnp.float32, math.log(0.0012), math.log(0.0024)))
    ranking = jax.vmap(permute_channels)(jax.random.split(key_pick, STACK_COUNT))
    quick_tally = P_SIZE // 2
    chosen_fast = ranking < quick_tally
    return jnp.where(chosen_fast, fast_rates, slow_rates)


def block_scale(stream_key, dims, cuts, smallest, high):
    loudness, own = 1.0, jax.random.fold_in(stream_key, 6)
    for position, blocks in cuts:
        steps = jnp.exp(jax.random.uniform(jax.random.fold_in(own, position), (blocks,), jnp.float32, smallest / len(cuts), high / len(cuts)))
        loudness = loudness * jnp.repeat(steps, dims[position] // blocks).reshape([-1 if axis == position else 1 for axis in range(len(dims))])
    return loudness


def centred(key, shape, deviation, most, cuts=(), dtype=jnp.bfloat16):
    entries = deviation * jax.random.normal(key, shape, jnp.float32)
    if cuts:
        entries = entries * block_scale(key, shape, cuts, -0.22, 0.18)
    return jnp.clip(entries, -most, most).astype(dtype)


def setup_inputs(seed: int = 0) -> dict:
    streams_of = jax.random.split(jax.random.key(seed), 7)
    return {
        "latents": centred(streams_of[0], (FRAMES, H, W, C), 1.0, 6.0, ((0, 8), (1, 4))),
        "frame_gaps": draw_frame_gaps(jax.random.fold_in(streams_of[6], 71), 0),
        "decay_rates": draw_decay_rates(jax.random.fold_in(streams_of[6], 71), 0),
        "input_kernel": centred(streams_of[3], (STACK_COUNT, 3, 3, C, P_SIZE), (9 * C) ** -0.5, 0.125),
        "output_kernel": centred(streams_of[4], (STACK_COUNT, 3, 3, P_SIZE, C), (9 * P_SIZE) ** -0.5, 0.125),
        "feedthrough": jnp.clip(jax.random.uniform(streams_of[5], (STACK_COUNT, C), jnp.float32, -1.0, 1.0), -1.0, 1.0),
    }


def convolve(inputs, kernel):
    frames, vertical_extent, columns, channels = inputs.shape
    padded = jnp.pad(inputs, ((0, 0), (1, 1), (1, 1), (0, 0)))
    summed = jnp.zeros((frames * vertical_extent * columns, kernel.shape[-1]), jnp.float32)
    for row_tap in range(3):
        for col_tap in range(3):
            window = padded[:, row_tap:row_tap + vertical_extent, col_tap:col_tap + columns, :].reshape(-1, channels)
            summed = summed + jnp.dot(window, kernel[row_tap, col_tap], preferred_element_type=jnp.float32)
    return summed.reshape(frames, vertical_extent, columns, -1)

def recurrence(driving, decays):

    def advance(carried, pieces):
        driven, factor = pieces
        carried = factor * carried + jnp.sqrt(1.0 - factor * factor) * driven
        return (carried, carried)
    initial = jnp.zeros(driving.shape[1:], jnp.float32)
    _, states = lax.scan(advance, initial, (driving, decays))
    return states

def reference(latents, frame_gaps, decay_rates, input_kernel, output_kernel, feedthrough):
    inputs = latents
    for layer_index in range(STACK_COUNT):
        decays = jnp.exp(-frame_gaps[:, None] * decay_rates[layer_index][None, :])
        driving = convolve(inputs, input_kernel[layer_index])
        states = recurrence(driving, decays).astype(jnp.bfloat16)
        premix = convolve(states, output_kernel[layer_index]) + feedthrough[layer_index] * inputs.astype(jnp.float32)
        inputs = jax.nn.gelu(premix, approximate=True).astype(jnp.bfloat16)
    return inputs
```

```python
import functools

import jax
import jax.numpy as jnp
from jax import lax
from jax.experimental import pallas as pl
from jax.experimental.pallas import tpu as pltpu
from jax.sharding import PartitionSpec as P

MESH = pl.DeviceIdType.MESH
F32 = jnp.float32
BF16 = jnp.bfloat16


def gelu(v):
    return 0.5 * v * (1.0 + jnp.tanh(0.7978845608028654 * (v + 0.044715 * (v * v * v))))


def kernel(
    n, bands, base, owners,
    lat, gaps, rates, feed, win, wout,
    out,
    x0, x1, xs, st, halo, wbuf, cums, dec_src, dec_box, fin, inbox, outbox, carry,
    lat_sem, w_sem, halo_send, halo_recv, dec_send, dec_recv, fin_send, fin_recv, car_send, car_recv,
):
    layers = win.shape[0]
    frames, rows, width, chans = lat.shape
    per_row = owners // rows
    share = width // per_row
    me = lax.axis_index("tm")
    band = lax.axis_index("rows")
    has_up = band > 0
    has_down = band < bands - 1
    is_owner = jnp.logical_and(me >= base, me < base + owners)
    my_share = me - base
    interior = list(range(1, rows - 1))
    edge = [0, rows - 1]
    pending = []

    def send(cond, src, dst, ssem, rsem, dev):
        copy = pltpu.make_async_remote_copy(
            src_ref=src, dst_ref=dst, send_sem=ssem, recv_sem=rsem, device_id=dev, device_id_type=MESH
        )
        pl.when(cond)(copy.start)
        pending.append((cond, copy))

    def receive(cond, dst, ssem, rsem, dev):
        copy = pltpu.make_async_remote_copy(
            src_ref=dst, dst_ref=dst, send_sem=ssem, recv_sem=rsem, device_id=dev, device_id_type=MESH
        )
        pl.when(cond)(copy.wait_recv)

    barrier = pltpu.get_barrier_semaphore()
    for step in range(1, n):
        pl.semaphore_signal(barrier, inc=1, device_id={"tm": lax.rem(me + step, n)}, device_id_type=MESH)

    @pl.when(has_up)
    def _():
        pl.semaphore_signal(barrier, inc=1, device_id={"rows": band - 1}, device_id_type=MESH)

    @pl.when(has_down)
    def _():
        pl.semaphore_signal(barrier, inc=1, device_id={"rows": band + 1}, device_id_type=MESH)

    row_copies = [pltpu.make_async_copy(lat.at[:, r], x0.at[r], lat_sem.at[r]) for r in range(rows)]
    for copy in row_copies:
        copy.start()
    w_copies = {}
    for layer in range(layers):
        for which, src in enumerate((win, wout)):
            copy = pltpu.make_async_copy(src.at[layer], wbuf.at[layer, which], w_sem.at[layer, which])
            copy.start()
            w_copies[layer, which] = copy

    decays = []
    for layer in range(layers):
        rate = rates[layer : layer + 1, :]
        factors = [jnp.exp(-gaps[t] * rate) for t in range(frames)]
        total = factors[0]
        cums[layer, 0:1, :] = total
        for t in range(1, frames):
            total = total * factors[t]
            cums[layer, t : t + 1, :] = total
        dec_src[layer : layer + 1, :] = total
        decays.append(factors)

    @pl.when(is_owner)
    def _():
        dec_box[me] = dec_src[...]

    @pl.when(jnp.logical_not(has_up))
    def _():
        for layer in range(layers):
            for which in range(2):
                halo[layer, which, 0] = jnp.zeros(halo.shape[3:], BF16)

    @pl.when(jnp.logical_not(has_down))
    def _():
        for layer in range(layers):
            for which in range(2):
                halo[layer, which, 1] = jnp.zeros(halo.shape[3:], BF16)

    @pl.when(me == 0)
    def _():
        carry[...] = jnp.zeros(carry.shape, BF16)

    pl.semaphore_wait(barrier, n - 1 + has_up.astype(jnp.int32) + has_down.astype(jnp.int32))

    def send_halo(layer, which, top, bottom):
        send(has_up, top, halo.at[layer, which, 1], halo_send.at[layer, which, 0],
             halo_recv.at[layer, which, 1], {"rows": band - 1})
        send(has_down, bottom, halo.at[layer, which, 0], halo_send.at[layer, which, 1],
             halo_recv.at[layer, which, 0], {"rows": band + 1})

    def wait_halo(layer, which):
        receive(has_up, halo.at[layer, which, 0], halo_send.at[layer, which, 0],
                halo_recv.at[layer, which, 0], {"rows": band - 1})
        receive(has_down, halo.at[layer, which, 1], halo_send.at[layer, which, 1],
                halo_recv.at[layer, which, 1], {"rows": band + 1})

    send_halo(0, 0, lat.at[:, 0], lat.at[:, rows - 1])
    for s in range(owners):
        send(jnp.logical_and(me < n - 1, me != base + s), dec_src, dec_box.at[me], dec_send.at[s],
             dec_recv.at[me], {"tm": base + s})

    def conv(x, layer, which, wanted):
        def row(i):
            if i < 0:
                v = halo[layer, which, 0]
            elif i == rows:
                v = halo[layer, which, 1]
            else:
                v = x[i]
            return v.reshape(frames * width, chans)

        lhs = [jnp.concatenate([row(i + a - 1) for i in wanted], axis=0) for a in range(3)]
        lhs = jnp.concatenate(lhs, axis=1)
        parts = []
        for b in range(3):
            rhs = jnp.concatenate([wbuf[layer, which, a, b] for a in range(3)], axis=0)
            parts.append(jnp.dot(lhs, rhs, preferred_element_type=F32))
        size = lhs.shape[0]
        column = lax.rem(lax.broadcasted_iota(jnp.int32, (size, parts[0].shape[1]), 0), width)
        left = jnp.where(column == 0, 0.0, pltpu.roll(parts[0], 1, 0))
        right = jnp.where(column == width - 1, 0.0, pltpu.roll(parts[2], size - 1, 0))
        return (parts[1] + left + right).reshape(len(wanted), frames, width, -1)

    def drive(x, layer, wanted):
        driven = conv(x, layer, 0, wanted)
        for j, r in enumerate(wanted):
            state = None
            for t in range(frames):
                factor = decays[layer][t]
                fresh = jnp.sqrt(1.0 - factor * factor) * driven[j, t]
                state = fresh if state is None else factor * state + fresh
                st[r, t] = state
            for piece in range(per_row):
                s = r * per_row + piece
                part = state[piece * share : (piece + 1) * share].astype(BF16)
                fin[layer, s] = part

                @pl.when(me == base + s)
                def _():
                    inbox[layer, me] = part

                send(jnp.logical_and(me < n - 1, me != base + s), fin.at[layer, s], inbox.at[layer, me],
                     fin_send.at[layer, s], fin_recv.at[layer, me], {"tm": base + s})

    def own(layer):
        total = None
        for k in range(1, n):
            receive(jnp.logical_and(is_owner, me != k - 1), inbox.at[layer, k - 1], fin_send.at[layer, 0],
                    fin_recv.at[layer, k - 1], {"tm": k - 1})
            if layer == 0:
                receive(jnp.logical_and(is_owner, me != k - 1), dec_box.at[k - 1], dec_send.at[0],
                        dec_recv.at[k - 1], {"tm": k - 1})
            last = inbox[layer, k - 1].astype(F32)
            total = last if total is None else dec_box[k - 1, layer : layer + 1, :] * total + last
            outbox[layer, k] = total.astype(BF16)

            @pl.when(jnp.logical_and(is_owner, me == k))
            def _():
                carry[layer, my_share] = outbox[layer, k]

            send(jnp.logical_and(is_owner, me != k), outbox.at[layer, k], carry.at[layer, my_share],
                 car_send.at[layer, k], car_recv.at[layer, my_share], {"tm": k})

    def finish(layer, r):
        pieces = []
        for piece in range(per_row):
            s = r * per_row + piece
            receive(jnp.logical_and(me > 0, me != base + s), carry.at[layer, s], car_send.at[layer, 0],
                    car_recv.at[layer, s], {"tm": base + s})
            pieces.append(carry[layer, s].astype(F32))
        incoming = pieces[0] if per_row == 1 else jnp.concatenate(pieces, axis=0)
        for t in range(frames):
            xs[layer, r, t] = (st[r, t] + cums[layer, t : t + 1, :] * incoming).astype(BF16)

    def mix(x, layer, wanted, put):
        mixed = conv(xs.at[layer], layer, 1, wanted)
        gain = feed[layer : layer + 1, :]
        for j, r in enumerate(wanted):
            skipped = x[r].astype(F32)
            put(r, gelu(mixed[j] + gain * skipped).astype(BF16))

    x = x0
    for copy in row_copies:
        copy.wait()
    for layer in range(layers):
        w_copies[layer, 0].wait()
        drive(x, layer, interior)
        wait_halo(layer, 0)
        drive(x, layer, edge)

        own(layer)

        finish(layer, 0)
        finish(layer, rows - 1)
        send_halo(layer, 1, xs.at[layer, 0], xs.at[layer, rows - 1])
        for r in interior:
            finish(layer, r)
        w_copies[layer, 1].wait()
        if layer == layers - 1:
            def put(r, v):
                out[:, r] = v
        else:
            def put(r, v, layer=layer):
                x1[layer, r] = v
        mix(x, layer, interior, put)
        wait_halo(layer, 1)
        mix(x, layer, edge, put)
        if layer < layers - 1:
            x = x1.at[layer]
            send_halo(layer + 1, 0, x.at[0], x.at[rows - 1])

    for cond, copy in pending:
        pl.when(cond)(copy.wait_send)


def per_device(n, bands, latents, frame_gaps, decay_rates, input_kernel, output_kernel, feedthrough):
    frames, rows, width, chans = latents.shape
    layers = input_kernel.shape[0]
    owners = n // 2
    base = n // 4
    share = rows * width // owners
    any_spec = pl.BlockSpec(memory_space=pl.ANY)
    vmem = pl.BlockSpec(memory_space=pltpu.VMEM)
    dma = pltpu.SemaphoreType.DMA
    return pl.pallas_call(
        functools.partial(kernel, n, bands, base, owners),
        out_shape=jax.ShapeDtypeStruct(latents.shape, BF16),
        in_specs=[any_spec, pl.BlockSpec(memory_space=pltpu.SMEM), vmem, vmem, any_spec, any_spec],
        out_specs=vmem,
        scratch_shapes=[
            pltpu.VMEM((rows, frames, width, chans), BF16),
            pltpu.VMEM((max(layers - 1, 1), rows, frames, width, chans), BF16),
            pltpu.VMEM((layers, rows, frames, width, chans), BF16),
            pltpu.VMEM((rows, frames, width, chans), F32),
            pltpu.VMEM((layers, 2, 2, frames, width, chans), BF16),
            pltpu.VMEM((layers, 2) + input_kernel.shape[1:], BF16),
            pltpu.VMEM((layers, frames, chans), F32),
            pltpu.VMEM((layers, chans), F32),
            pltpu.VMEM((n, layers, chans), F32),
            pltpu.VMEM((layers, owners, share, chans), BF16),
            pltpu.VMEM((layers, n, share, chans), BF16),
            pltpu.VMEM((layers, n, share, chans), BF16),
            pltpu.VMEM((layers, owners, share, chans), BF16),
            dma((rows,)),
            dma((layers, 2)),
            dma((layers, 2, 2)),
            dma((layers, 2, 2)),
            dma((owners,)),
            dma((n,)),
            dma((layers, owners)),
            dma((layers, n)),
            dma((layers, n)),
            dma((layers, owners)),
        ],
        compiler_params=pltpu.CompilerParams(collective_id=0, has_side_effects=True),
    )(latents, frame_gaps, decay_rates, feedthrough, input_kernel, output_kernel)


def solution(mesh):
    in_specs = (P("tm", "rows", None, None), P("tm"), P(), P(), P(), P())
    out_specs = P("tm", "rows", None, None)
    return jax.shard_map(
        functools.partial(per_device, mesh.shape["tm"], mesh.shape["rows"]),
        mesh=mesh, in_specs=in_specs, out_specs=out_specs, check_vma=False,
    )
```

```python
import functools

import jax
import jax.numpy as jnp
from jax import lax
from jax.experimental import pallas as pl
from jax.experimental.pallas import tpu as pltpu
from jax.sharding import PartitionSpec as P

MESH = pl.DeviceIdType.MESH
F32 = jnp.float32
BF16 = jnp.bfloat16


def gelu(v):
    return 0.5 * v * (1.0 + jnp.tanh(0.7978845608028654 * (v + 0.044715 * (v * v * v))))


def fold(v):
    half = v.shape[-1] // 2
    return jnp.concatenate([v[..., :half], v[..., half:]], axis=-2)


def unfold(v):
    half = v.shape[-2] // 2
    return jnp.concatenate([v[..., :half, :], v[..., half:, :]], axis=-1)


def kernel(
    n, bands, base, owners,
    lat, gaps, rates, feed, win, wout,
    out,
    x0, x1, xs, xh, st, sth, halo, wbuf, cums, dec_src, dec_box, fin, inbox, outbox, carry, hcarry,
    lat_sem, w_sem, halo_send, halo_recv, dec_send, dec_recv, fin_send, fin_recv, car_send, car_recv,
    hcar_send, hcar_recv,
):
    layers = win.shape[0]
    frames, rows, width, chans = lat.shape
    share = width // owners
    me = lax.axis_index("tm")
    band = lax.axis_index("rows")
    has_up = band > 0
    has_down = band < bands - 1
    is_owner = jnp.logical_and(me >= base, me < base + owners)
    my_share = lax.rem(me + owners * n - base, owners)
    groups = [list(range(1, rows - 1)), [0, rows - 1]]
    sides = [(has_up, lax.rem(band + bands - 1, bands)), (has_down, lax.rem(band + 1, bands))]
    pending = []

    def both(*conds):
        return functools.reduce(jnp.logical_and, conds)

    def send(cond, src, dst, ssem, rsem, dev):
        copy = pltpu.make_async_remote_copy(
            src_ref=src, dst_ref=dst, send_sem=ssem, recv_sem=rsem, device_id=dev, device_id_type=MESH
        )
        pl.when(cond)(copy.start)
        pending.append((cond, copy))

    def receive(cond, dst, ssem, rsem, dev):
        copy = pltpu.make_async_remote_copy(
            src_ref=dst, dst_ref=dst, send_sem=ssem, recv_sem=rsem, device_id=dev, device_id_type=MESH
        )
        pl.when(cond)(copy.wait_recv)

    barrier = pltpu.get_barrier_semaphore()

    def greet(cond, dev):
        @pl.when(cond)
        def _():
            pl.semaphore_signal(barrier, inc=1, device_id=dev, device_id_type=MESH)

    for there, other in sides:
        for s in range(owners):
            greet(there, {"tm": base + s, "rows": other})
        greet(both(there, jnp.logical_not(is_owner)), {"rows": other})
    for k in range(n):
        if base <= k < base + owners:
            greet(me != k, {"tm": k})
        else:
            greet(is_owner, {"tm": k})

    row_copies = [pltpu.make_async_copy(lat.at[:, r], x0.at[r], lat_sem.at[r]) for r in range(rows)]
    for copy in row_copies:
        copy.start()
    w_copies = {}
    for layer in range(layers):
        for which, src in enumerate((win, wout)):
            copy = pltpu.make_async_copy(src.at[layer], wbuf.at[layer, which], w_sem.at[layer, which])
            copy.start()
            w_copies[layer, which] = copy

    decays = []
    for layer in range(layers):
        rate = rates[layer : layer + 1, :]
        factors = [jnp.exp(-gaps[t] * rate) for t in range(frames)]
        total = factors[0]
        cums[layer, 0:1, :] = total
        for t in range(1, frames):
            total = total * factors[t]
            cums[layer, t : t + 1, :] = total
        dec_src[layer : layer + 1, :] = total
        decays.append(factors)

    @pl.when(is_owner)
    def _():
        dec_box[me] = dec_src[...]

    for d, (there, _other) in enumerate(sides):
        @pl.when(jnp.logical_not(there))
        def _():
            for layer in range(layers):
                for which in range(2):
                    halo[layer, which, d] = jnp.zeros(halo.shape[3:], BF16)

        @pl.when(jnp.logical_or(me == 0, jnp.logical_not(there)))
        def _():
            for layer in range(layers):
                hcarry[layer, d] = jnp.zeros(hcarry.shape[2:], BF16)

    @pl.when(me == 0)
    def _():
        carry[...] = jnp.zeros(carry.shape, BF16)

    neighbours = has_up.astype(jnp.int32) + has_down.astype(jnp.int32)
    pl.semaphore_wait(
        barrier, jnp.where(is_owner, n - 1 + neighbours * n, owners + neighbours)
    )

    def send_halo(layer, which, top, bottom):
        for d, (src, (there, other)) in enumerate(zip((top, bottom), sides)):
            send(there, src, halo.at[layer, which, 1 - d], halo_send.at[layer, which, d],
                 halo_recv.at[layer, which, 1 - d], {"rows": other})

    def wait_halo(layer, which):
        for d, (there, other) in enumerate(sides):
            receive(there, halo.at[layer, which, d], halo_send.at[layer, which, d],
                    halo_recv.at[layer, which, d], {"rows": other})

    send_halo(0, 0, lat.at[:, 0], lat.at[:, rows - 1])
    for s in range(owners):
        send(both(me < n - 1, me != base + s), dec_src, dec_box.at[me], dec_send.at[s],
             dec_recv.at[me], {"tm": base + s})

    def conv(x, beyond, weights, wanted):
        def row(i):
            v = beyond(0) if i < 0 else beyond(1) if i == rows else x(i)
            return v.reshape(frames * width, chans)

        lhs = [jnp.concatenate([row(i + a - 1) for i in wanted], axis=0) for a in range(3)]
        lhs = jnp.concatenate(lhs, axis=1)
        parts = []
        for b in range(3):
            rhs = jnp.concatenate([weights(a, b) for a in range(3)], axis=0)
            parts.append(jnp.dot(lhs, rhs, preferred_element_type=F32))
        size = lhs.shape[0]
        column = lax.rem(lax.broadcasted_iota(jnp.int32, (size, parts[0].shape[1]), 0), width)
        left = jnp.where(column == 0, 0.0, pltpu.roll(parts[0], 1, 0))
        right = jnp.where(column == width - 1, 0.0, pltpu.roll(parts[2], size - 1, 0))
        return (parts[1] + left + right).reshape(len(wanted), frames, width, -1)

    def drive(x, layer, g):
        driven = conv(x, lambda d: halo[layer, 0, d], lambda a, b: wbuf[layer, 0, a, b], groups[g])
        for j, r in enumerate(groups[g]):
            state = None
            for t in range(frames):
                factor = decays[layer][t]
                fresh = jnp.sqrt(1.0 - factor * factor) * driven[j, t]
                state = fresh if state is None else factor * state + fresh
                st[r, t] = state
                if g == 1:
                    sth[layer, j, t] = state.astype(BF16)
            for s in range(owners):
                fin[layer, g, s, j] = fold(state[s * share : (s + 1) * share]).astype(BF16)
        for s in range(owners):
            @pl.when(me == base + s)
            def _():
                inbox[layer, g, me] = fin[layer, g, s]

            send(both(me < n - 1, me != base + s), fin.at[layer, g, s], inbox.at[layer, g, me],
                 fin_send.at[layer, g, s], fin_recv.at[layer, g, me], {"tm": base + s})
        if g == 1:
            send_halo(layer, 1, sth.at[layer, 0], sth.at[layer, 1])

    def own(layer, g):
        total = None
        for k in range(1, n):
            other = both(is_owner, me != k - 1)
            receive(other, inbox.at[layer, g, k - 1], fin_send.at[layer, g, 0],
                    fin_recv.at[layer, g, k - 1], {"tm": k - 1})
            if layer == 0 and g == 0:
                receive(other, dec_box.at[k - 1], dec_send.at[0], dec_recv.at[k - 1], {"tm": k - 1})
            last = unfold(inbox[layer, g, k - 1].astype(F32))
            total = last if total is None else dec_box[k - 1, layer : layer + 1, :] * total + last
            outbox[layer, g, k] = fold(total).astype(BF16)

            if g == 1:
                for d, (there, band_to) in enumerate(sides):
                    send(both(is_owner, there), outbox.at[layer, g, k, d], hcarry.at[layer, 1 - d, my_share],
                         hcar_send.at[layer, d, k], hcar_recv.at[layer, 1 - d, my_share],
                         {"tm": k, "rows": band_to})
            send(both(is_owner, me != k), outbox.at[layer, g, k], carry.at[layer, g, my_share],
                 car_send.at[layer, g, k], car_recv.at[layer, g, my_share], {"tm": k})

            @pl.when(both(is_owner, me == k))
            def _():
                carry[layer, g, my_share] = outbox[layer, g, k]

    def finish(layer, g):
        for s in range(owners):
            receive(both(me > 0, me != base + s), carry.at[layer, g, s], car_send.at[layer, g, 0],
                    car_recv.at[layer, g, s], {"tm": base + s})
        for j, r in enumerate(groups[g]):
            incoming = jnp.concatenate([unfold(carry[layer, g, s, j].astype(F32)) for s in range(owners)], axis=0)
            for t in range(frames):
                xs[layer, r, t] = (st[r, t] + cums[layer, t : t + 1, :] * incoming).astype(BF16)

    def finish_halo(layer):
        wait_halo(layer, 1)
        for d, (there, band_to) in enumerate(sides):
            for s in range(owners):
                receive(both(me > 0, there), hcarry.at[layer, d, s], hcar_send.at[layer, d, 0],
                        hcar_recv.at[layer, d, s], {"tm": base + s, "rows": band_to})
            incoming = jnp.concatenate([unfold(hcarry[layer, d, s].astype(F32)) for s in range(owners)], axis=0)
            for t in range(frames):
                local = halo[layer, 1, d, t].astype(F32)
                xh[layer, d, t] = (local + cums[layer, t : t + 1, :] * incoming).astype(BF16)

    def mix(x, layer, wanted, put):
        mixed = conv(lambda r: xs[layer, r], lambda d: xh[layer, d], lambda a, b: wbuf[layer, 1, a, b], wanted)
        gain = feed[layer : layer + 1, :]
        for j, r in enumerate(wanted):
            skipped = x(r).astype(F32)
            put(r, gelu(mixed[j] + gain * skipped).astype(BF16))

    x = lambda r: x0[r]
    for copy in row_copies:
        copy.wait()
    for layer in range(layers):
        w_copies[layer, 0].wait()
        drive(x, layer, 0)
        wait_halo(layer, 0)
        drive(x, layer, 1)
        for g in range(2):
            own(layer, g)
        for g in range(2):
            finish(layer, g)
        finish_halo(layer)
        w_copies[layer, 1].wait()
        if layer == layers - 1:
            def put(r, v):
                out[:, r] = v

            mix(x, layer, list(range(rows)), put)
        else:
            def put(r, v):
                x1[layer, r] = v

            mix(x, layer, groups[1], put)
            send_halo(layer + 1, 0, x1.at[layer, 0], x1.at[layer, rows - 1])
            mix(x, layer, groups[0], put)
            x = functools.partial(lambda layer, r: x1[layer, r], layer)

    for cond, copy in pending:
        pl.when(cond)(copy.wait_send)


def per_device(n, bands, latents, frame_gaps, decay_rates, input_kernel, output_kernel, feedthrough):
    frames, rows, width, chans = latents.shape
    layers = input_kernel.shape[0]
    owners = min(n // 2, max(width // 8, 1))
    base = n // 2 - owners // 2
    share = width // owners
    most = max(rows - 2, 2)
    any_spec = pl.BlockSpec(memory_space=pl.ANY)
    vmem = pl.BlockSpec(memory_space=pltpu.VMEM)
    dma = pltpu.SemaphoreType.DMA
    return pl.pallas_call(
        functools.partial(kernel, n, bands, base, owners),
        out_shape=jax.ShapeDtypeStruct(latents.shape, BF16),
        in_specs=[any_spec, pl.BlockSpec(memory_space=pltpu.SMEM), vmem, vmem, any_spec, any_spec],
        out_specs=vmem,
        scratch_shapes=[
            pltpu.VMEM((rows, frames, width, chans), BF16),
            pltpu.VMEM((max(layers - 1, 1), rows, frames, width, chans), BF16),
            pltpu.VMEM((layers, rows, frames, width, chans), BF16),
            pltpu.VMEM((layers, 2, frames, width, chans), BF16),
            pltpu.VMEM((rows, frames, width, chans), F32),
            pltpu.VMEM((layers, 2, frames, width, chans), BF16),
            pltpu.VMEM((layers, 2, 2, frames, width, chans), BF16),
            pltpu.VMEM((layers, 2) + input_kernel.shape[1:], BF16),
            pltpu.VMEM((layers, frames, chans), F32),
            pltpu.VMEM((layers, chans), F32),
            pltpu.VMEM((n, layers, chans), F32),
            pltpu.VMEM((layers, 2, owners, most, 2 * share, chans // 2), BF16),
            pltpu.VMEM((layers, 2, n, most, 2 * share, chans // 2), BF16),
            pltpu.VMEM((layers, 2, n, most, 2 * share, chans // 2), BF16),
            pltpu.VMEM((layers, 2, owners, most, 2 * share, chans // 2), BF16),
            pltpu.VMEM((layers, 2, owners, 2 * share, chans // 2), BF16),
            dma((rows,)),
            dma((layers, 2)),
            dma((layers, 2, 2)),
            dma((layers, 2, 2)),
            dma((owners,)),
            dma((n,)),
            dma((layers, 2, owners)),
            dma((layers, 2, n)),
            dma((layers, 2, n)),
            dma((layers, 2, owners)),
            dma((layers, 2, n)),
            dma((layers, 2, owners)),
        ],
        compiler_params=pltpu.CompilerParams(collective_id=0, has_side_effects=True),
    )(latents, frame_gaps, decay_rates, feedthrough, input_kernel, output_kernel)


def solution(mesh):
    in_specs = (P("tm", "rows", None, None), P("tm"), P(), P(), P(), P())
    out_specs = P("tm", "rows", None, None)
    return jax.shard_map(
        functools.partial(per_device, mesh.shape["tm"], mesh.shape["rows"]),
        mesh=mesh, in_specs=in_specs, out_specs=out_specs, check_vma=False,
    )
```

```python
import functools

import jax
import jax.numpy as jnp
from jax import lax
from jax.experimental import pallas as pl
from jax.experimental.pallas import tpu as pltpu
from jax.sharding import PartitionSpec as P

MESH = pl.DeviceIdType.MESH
F32 = jnp.float32
BF16 = jnp.bfloat16


def gelu(v):
    return 0.5 * v * (1.0 + jnp.tanh(0.7978845608028654 * (v + 0.044715 * (v * v * v))))


def fold(v):
    half = v.shape[-1] // 2
    return jnp.concatenate([v[..., :half], v[..., half:]], axis=-2)


def unfold(v):
    half = v.shape[-2] // 2
    return jnp.concatenate([v[..., :half, :], v[..., half:, :]], axis=-1)


def kernel(
    n, bands, base, owners,
    lat, gaps, rates, feed, win, wout,
    out,
    x0, x1, xs, xh, st, sth, halo, wbuf, cums, dec_src, dec_box, fin, inbox, outbox, carry, hcarry,
    lat_sem, w_sem, halo_send, halo_recv, dec_send, dec_recv, fin_send, fin_recv, car_send, car_recv,
    hcar_send, hcar_recv,
):
    layers = win.shape[0]
    frames, rows, width, chans = lat.shape
    share = width // owners
    me = lax.axis_index("tm")
    band = lax.axis_index("rows")
    has_up = band > 0
    has_down = band < bands - 1
    is_owner = jnp.logical_and(me >= base, me < base + owners)
    my_share = lax.rem(me + owners * n - base, owners)
    groups = [list(range(1, rows - 1)), [0, rows - 1]]
    sides = [(has_up, lax.rem(band + bands - 1, bands)), (has_down, lax.rem(band + 1, bands))]
    pending = []

    def both(*conds):
        return functools.reduce(jnp.logical_and, conds)

    def send(cond, src, dst, ssem, rsem, dev):
        copy = pltpu.make_async_remote_copy(
            src_ref=src, dst_ref=dst, send_sem=ssem, recv_sem=rsem, device_id=dev, device_id_type=MESH
        )
        pl.when(cond)(copy.start)
        pending.append((cond, copy))

    def receive(cond, dst, ssem, rsem, dev):
        copy = pltpu.make_async_remote_copy(
            src_ref=dst, dst_ref=dst, send_sem=ssem, recv_sem=rsem, device_id=dev, device_id_type=MESH
        )
        pl.when(cond)(copy.wait_recv)

    barrier = pltpu.get_barrier_semaphore()

    def greet(cond, dev):
        @pl.when(cond)
        def _():
            pl.semaphore_signal(barrier, inc=1, device_id=dev, device_id_type=MESH)

    for there, other in sides:
        for s in range(owners):
            greet(there, {"tm": base + s, "rows": other})
        greet(both(there, jnp.logical_not(is_owner)), {"rows": other})
    for k in range(n):
        if base <= k < base + owners:
            greet(me != k, {"tm": k})
        else:
            greet(is_owner, {"tm": k})

    row_copies = [pltpu.make_async_copy(lat.at[:, r], x0.at[r], lat_sem.at[r]) for r in range(rows)]
    for copy in row_copies:
        copy.start()
    w_copies = {}
    for layer in range(layers):
        for which, src in enumerate((win, wout)):
            copy = pltpu.make_async_copy(src.at[layer], wbuf.at[layer, which], w_sem.at[layer, which])
            copy.start()
            w_copies[layer, which] = copy

    decays = []
    for layer in range(layers):
        rate = rates[layer : layer + 1, :]
        factors = [jnp.exp(-gaps[t] * rate) for t in range(frames)]
        total = factors[0]
        cums[layer, 0:1, :] = total
        for t in range(1, frames):
            total = total * factors[t]
            cums[layer, t : t + 1, :] = total
        dec_src[layer : layer + 1, :] = total
        decays.append(factors)

    @pl.when(is_owner)
    def _():
        dec_box[me] = dec_src[...]

    for d, (there, _other) in enumerate(sides):
        @pl.when(jnp.logical_not(there))
        def _():
            for layer in range(layers):
                for which in range(2):
                    halo[layer, which, d] = jnp.zeros(halo.shape[3:], BF16)

        @pl.when(jnp.logical_or(me == 0, jnp.logical_not(there)))
        def _():
            for layer in range(layers):
                hcarry[layer, d] = jnp.zeros(hcarry.shape[2:], BF16)

    @pl.when(me == 0)
    def _():
        carry[...] = jnp.zeros(carry.shape, BF16)

    neighbours = has_up.astype(jnp.int32) + has_down.astype(jnp.int32)
    pl.semaphore_wait(
        barrier, jnp.where(is_owner, n - 1 + neighbours * n, owners + neighbours)
    )

    def send_halo(layer, which, top, bottom):
        for d, (src, (there, other)) in enumerate(zip((top, bottom), sides)):
            send(there, src, halo.at[layer, which, 1 - d], halo_send.at[layer, which, d],
                 halo_recv.at[layer, which, 1 - d], {"rows": other})

    def wait_halo(layer, which):
        for d, (there, other) in enumerate(sides):
            receive(there, halo.at[layer, which, d], halo_send.at[layer, which, d],
                    halo_recv.at[layer, which, d], {"rows": other})

    send_halo(0, 0, lat.at[:, 0], lat.at[:, rows - 1])
    for s in range(owners):
        send(both(me < n - 1, me != base + s), dec_src, dec_box.at[me], dec_send.at[s],
             dec_recv.at[me], {"tm": base + s})

    def conv(x, beyond, weights, wanted):
        def row(i):
            v = beyond(0) if i < 0 else beyond(1) if i == rows else x(i)
            return v.reshape(frames * width, chans)

        lhs = [jnp.concatenate([row(i + a - 1) for i in wanted], axis=0) for a in range(3)]
        lhs = jnp.concatenate(lhs, axis=1)
        parts = []
        for b in range(3):
            rhs = jnp.concatenate([weights(a, b) for a in range(3)], axis=0)
            parts.append(jnp.dot(lhs, rhs, preferred_element_type=F32))
        size = lhs.shape[0]
        column = lax.rem(lax.broadcasted_iota(jnp.int32, (size, parts[0].shape[1]), 0), width)
        left = jnp.where(column == 0, 0.0, pltpu.roll(parts[0], 1, 0))
        right = jnp.where(column == width - 1, 0.0, pltpu.roll(parts[2], size - 1, 0))
        return (parts[1] + left + right).reshape(len(wanted), frames, width, -1)

    def drive(x, layer, g):
        driven = conv(x, lambda d: halo[layer, 0, d], lambda a, b: wbuf[layer, 0, a, b], groups[g])
        for j, r in enumerate(groups[g]):
            state = None
            for t in range(frames):
                factor = decays[layer][t]
                fresh = jnp.sqrt(1.0 - factor * factor) * driven[j, t]
                state = fresh if state is None else factor * state + fresh
                st[r, t] = state
                if g == 1:
                    sth[layer, j, t] = state.astype(BF16)
            for s in range(owners):
                fin[layer, g, s, j] = fold(state[s * share : (s + 1) * share]).astype(BF16)
        for s in range(owners):
            @pl.when(me == base + s)
            def _():
                inbox[layer, g, me] = fin[layer, g, s]

            send(both(me < n - 1, me != base + s), fin.at[layer, g, s], inbox.at[layer, g, me],
                 fin_send.at[layer, g, s], fin_recv.at[layer, g, me], {"tm": base + s})
        if g == 1:
            send_halo(layer, 1, sth.at[layer, 0], sth.at[layer, 1])

    def own(layer, g):
        total = None
        for k in range(1, n):
            other = both(is_owner, me != k - 1)
            receive(other, inbox.at[layer, g, k - 1], fin_send.at[layer, g, 0],
                    fin_recv.at[layer, g, k - 1], {"tm": k - 1})
            if layer == 0 and g == 0:
                receive(other, dec_box.at[k - 1], dec_send.at[0], dec_recv.at[k - 1], {"tm": k - 1})
            last = unfold(inbox[layer, g, k - 1].astype(F32))
            total = last if total is None else dec_box[k - 1, layer : layer + 1, :] * total + last
            outbox[layer, g, k] = fold(total).astype(BF16)

            if g == 1:
                for d, (there, band_to) in enumerate(sides):
                    send(both(is_owner, there), outbox.at[layer, g, k, d], hcarry.at[layer, 1 - d, my_share],
                         hcar_send.at[layer, d, k], hcar_recv.at[layer, 1 - d, my_share],
                         {"tm": k, "rows": band_to})
            send(both(is_owner, me != k), outbox.at[layer, g, k], carry.at[layer, g, my_share],
                 car_send.at[layer, g, k], car_recv.at[layer, g, my_share], {"tm": k})

            @pl.when(both(is_owner, me == k))
            def _():
                carry[layer, g, my_share] = outbox[layer, g, k]

    def finish(layer, g):
        for s in range(owners):
            receive(both(me > 0, me != base + s), carry.at[layer, g, s], car_send.at[layer, g, 0],
                    car_recv.at[layer, g, s], {"tm": base + s})
        for j, r in enumerate(groups[g]):
            incoming = jnp.concatenate([unfold(carry[layer, g, s, j].astype(F32)) for s in range(owners)], axis=0)
            for t in range(frames):
                xs[layer, r, t] = (st[r, t] + cums[layer, t : t + 1, :] * incoming).astype(BF16)

    def finish_halo(layer):
        wait_halo(layer, 1)
        for d, (there, band_to) in enumerate(sides):
            for s in range(owners):
                receive(both(me > 0, there), hcarry.at[layer, d, s], hcar_send.at[layer, d, 0],
                        hcar_recv.at[layer, d, s], {"tm": base + s, "rows": band_to})
            incoming = jnp.concatenate([unfold(hcarry[layer, d, s].astype(F32)) for s in range(owners)], axis=0)
            for t in range(frames):
                local = halo[layer, 1, d, t].astype(F32)
                xh[layer, d, t] = (local + cums[layer, t : t + 1, :] * incoming).astype(BF16)

    def mix(x, layer, wanted, put):
        mixed = conv(lambda r: xs[layer, r], lambda d: xh[layer, d], lambda a, b: wbuf[layer, 1, a, b], wanted)
        gain = feed[layer : layer + 1, :]
        for j, r in enumerate(wanted):
            skipped = x(r).astype(F32)
            put(r, gelu(mixed[j] + gain * skipped).astype(BF16))

    x = lambda r: x0[r]
    for copy in row_copies:
        copy.wait()
    for layer in range(layers):
        w_copies[layer, 0].wait()
        drive(x, layer, 0)
        wait_halo(layer, 0)
        drive(x, layer, 1)
        for g in range(2):
            own(layer, g)
        for g in range(2):
            finish(layer, g)
        finish_halo(layer)
        w_copies[layer, 1].wait()
        if layer == layers - 1:
            def put(r, v):
                out[:, r] = v

            mix(x, layer, list(range(rows)), put)
        else:
            def put(r, v):
                x1[layer, r] = v

            mix(x, layer, groups[1], put)
            send_halo(layer + 1, 0, x1.at[layer, 0], x1.at[layer, rows - 1])
            mix(x, layer, groups[0], put)
            x = functools.partial(lambda layer, r: x1[layer, r], layer)

    for cond, copy in pending:
        pl.when(cond)(copy.wait_send)


def per_device(n, bands, latents, frame_gaps, decay_rates, input_kernel, output_kernel, feedthrough):
    frames, rows, width, chans = latents.shape
    layers = input_kernel.shape[0]
    owners = min(n // 2, max(width // 8, 1))
    base = n // 2 - owners // 2
    share = width // owners
    most = max(rows - 2, 2)
    any_spec = pl.BlockSpec(memory_space=pltpu.HBM)
    vmem = pl.BlockSpec(memory_space=pltpu.VMEM)
    dma = pltpu.SemaphoreType.DMA
    return pl.pallas_call(
        functools.partial(kernel, n, bands, base, owners),
        out_shape=pltpu.VMEM(latents.shape, BF16),
        in_specs=[any_spec, pl.BlockSpec(memory_space=pltpu.SMEM), vmem, vmem, any_spec, any_spec],
        out_specs=vmem,
        scratch_shapes=[
            pltpu.VMEM((rows, frames, width, chans), BF16),
            pltpu.VMEM((max(layers - 1, 1), rows, frames, width, chans), BF16),
            pltpu.VMEM((layers, rows, frames, width, chans), BF16),
            pltpu.VMEM((layers, 2, frames, width, chans), BF16),
            pltpu.VMEM((rows, frames, width, chans), F32),
            pltpu.VMEM((layers, 2, frames, width, chans), BF16),
            pltpu.VMEM((layers, 2, 2, frames, width, chans), BF16),
            pltpu.VMEM((layers, 2) + input_kernel.shape[1:], BF16),
            pltpu.VMEM((layers, frames, chans), F32),
            pltpu.VMEM((layers, chans), F32),
            pltpu.VMEM((n, layers, chans), F32),
            pltpu.VMEM((layers, 2, owners, most, 2 * share, chans // 2), BF16),
            pltpu.VMEM((layers, 2, n, most, 2 * share, chans // 2), BF16),
            pltpu.VMEM((layers, 2, n, most, 2 * share, chans // 2), BF16),
            pltpu.VMEM((layers, 2, owners, most, 2 * share, chans // 2), BF16),
            pltpu.VMEM((layers, 2, owners, 2 * share, chans // 2), BF16),
            dma((rows,)),
            dma((layers, 2)),
            dma((layers, 2, 2)),
            dma((layers, 2, 2)),
            dma((owners,)),
            dma((n,)),
            dma((layers, 2, owners)),
            dma((layers, 2, n)),
            dma((layers, 2, n)),
            dma((layers, 2, owners)),
            dma((layers, 2, n)),
            dma((layers, 2, owners)),
        ],
        compiler_params=pltpu.CompilerParams(collective_id=0, has_side_effects=True, vmem_limit_bytes=60 * 1024 * 1024),
    )(latents, frame_gaps, decay_rates, feedthrough, input_kernel, output_kernel)


def solution(mesh):
    in_specs = (P("tm", "rows", None, None), P("tm"), P(), P(), P(), P())
    out_specs = P("tm", "rows", None, None)
    return jax.shard_map(
        functools.partial(per_device, mesh.shape["tm"], mesh.shape["rows"]),
        mesh=mesh, in_specs=in_specs, out_specs=out_specs, check_vma=False,
    )
```
